32 devices in a mesh: grp: 4 (over z), row: 8 (over y, x, core).
Axes of the slice: x: 2, y: 2, z: 4, core: 2. Of those that a mesh axis runs over, the one named last changes fastest.
Arguments:
- theta: bfloat16 [8, 2048, 2048], P(None, ('row', 'grp')), may hold values from -6 to 6
- group_of: int32 [8], replicated, may hold values from 0 to 3, as said below
- sector_sizes: int32 [8], replicated, may hold values from 64 to 1024, as said below
- row_order: int32 [2048], P(('row', 'grp')), may hold values from 0 to 2047, as said below
- omega: bfloat16 [8, 2048, 1024], P('grp'), may hold values from -0.125 to 0.125
Outputs:
- basis: float32 [8, 2048, 1024], P('grp', 'row')
- core: float32 [2048, 8, 1024], P('row', 'grp')
The draws below stay inside these ranges and needn't reach their ends.
Inputs may be any that keep to these rules, and one draw needn't show every extreme that they name: `group_of`: each group number is named by exactly 2 sectors. `sector_sizes`: some sector has 1024 states and some has 64. `row_order`: each aligned block of 64 entries is a permutation of that block's own row numbers.
All inputs are finite; a program needn't handle non-finite values.
Results may differ from the reference program's by a relative error of at most 0.0028.
Values may be sent and summed in bfloat16 or wider, within the bound.
A program may use at most 128 MiB of HBM per device.

```python
import jax
import jax.numpy as jnp
from jax import lax

KMAX = 1024
COLS = 2048
SEC_GRP = 2
LR = 64
NSEC = 8
ROWS = 2048


def draw_group_of(key, part):
    shuffled = jax.random.permutation(jax.random.fold_in(key, 11), NSEC)
    return (shuffled // SEC_GRP).astype(jnp.int32)


def draw_sector_sizes(key, part):
    widths = jax.random.randint(jax.random.fold_in(key, 21), (NSEC,), KMAX // 16, KMAX + 1)
    chosen = jax.random.permutation(jax.random.fold_in(key, 22), NSEC)
    widths = widths.at[chosen[0]].set(KMAX)
    widths = widths.at[chosen[1]].set(KMAX // 16)
    return widths.astype(jnp.int32)


def shuffle_block(block_key):
    return jax.random.permutation(block_key, LR)


def draw_row_order(key, part):
    block_total = ROWS // LR
    sub_keys = jax.random.split(jax.random.fold_in(key, 31), block_total)
    shuffles = jax.vmap(shuffle_block)(sub_keys)
    offsets = jnp.arange(block_total, dtype=jnp.int32)[:, None] * LR
    return (shuffles.astype(jnp.int32) + offsets).reshape(ROWS).astype(jnp.int32)


def level_of(rng, extent, cuts, smallest, top_value):
    def one(axis_at, shards_of):
        draws = jax.random.uniform(jax.random.fold_in(jax.random.fold_in(rng, 6), axis_at), (shards_of,), jnp.float32, smallest / len(cuts), top_value / len(cuts))
        return jnp.repeat(jnp.exp(draws), extent[axis_at] // shards_of).reshape((-1,) + (1,) * (len(extent) - axis_at - 1))

    level = one(*cuts[0])
    for cut in cuts[1:]:
        level = level * one(*cut)
    return level


def normal_values(key, extent, deviation, bound, pieces=(), held_as=jnp.bfloat16):
    values = jax.random.normal(key, extent, jnp.float32) * deviation
    if len(pieces) > 0:
        values = level_of(key, extent, pieces, -0.22, 0.18) * values
    return jnp.clip(values, min=-bound, max=bound).astype(held_as)


def setup_inputs(seed: int = 0) -> dict:
    keys = jax.random.split(jax.random.key(seed), 6)
    return {
        "theta": normal_values(keys[0], (NSEC, ROWS, COLS), 1.0, 6.0, ((1, 32),)),
        "group_of": draw_group_of(jax.random.fold_in(keys[5], 71), 0),
        "sector_sizes": draw_sector_sizes(jax.random.fold_in(keys[5], 71), 0),
        "row_order": draw_row_order(jax.random.fold_in(keys[5], 71), 0),
        "omega": normal_values(keys[4], (NSEC, COLS, KMAX), COLS ** -0.5, 0.125, ((0, 4),)),
    }


def reference(theta, group_of, sector_sizes, row_order, omega):
    sorted_ids = jnp.argsort(group_of, stable=True).astype(jnp.int32)
    widths = jnp.take(sector_sizes, sorted_ids).astype(jnp.int32)

    def per_sector(inputs):
        sector_id, width, sketch_cols = inputs
        sector_rows = jnp.take(jnp.take(theta, sector_id, axis=0), row_order, axis=0)
        sketch = jnp.dot(sector_rows.astype(jnp.float32), sketch_cols.astype(jnp.float32), preferred_element_type=jnp.float32)
        live_cols = jnp.arange(sketch_cols.shape[1], dtype=jnp.int32) < width
        sketch = jnp.where(live_cols[None, :], sketch, jnp.zeros_like(sketch))
        gram = jnp.dot(sketch.T.astype(jnp.float32), sketch.astype(jnp.float32), precision=lax.Precision.HIGHEST, preferred_element_type=jnp.float32)
        gram = gram + jnp.diag(jnp.where(live_cols, 0.0, 1.0).astype(gram.dtype))
        lower = jnp.linalg.cholesky(gram)
        basis = lax.linalg.triangular_solve(lower, sketch, left_side=False, lower=True, transpose_a=True)
        wide_rows = sector_rows.astype(jnp.float32)
        core = jnp.dot(wide_rows.T.astype(jnp.float32), basis.astype(jnp.float32), precision=lax.Precision.HIGHEST, preferred_element_type=jnp.float32)
        return (basis, core)
    basis, core = lax.map(per_sector, (sorted_ids, widths, omega))
    return (basis, jnp.transpose(core, (1, 0, 2)))
```

```python
import jax
import jax.numpy as jnp
from jax import lax
from jax.experimental import pallas as pl
from jax.experimental.pallas import tpu as pltpu
from jax.sharding import PartitionSpec as P

BLK = 128
HI = lax.Precision.HIGHEST


def factor_tile(tiles):
    sub = lax.broadcasted_iota(jnp.int32, (8, BLK), 0)
    lane = lax.broadcasted_iota(jnp.int32, (8, BLK), 1)
    count = BLK // 8
    rows = [[t[8 * i:8 * i + 8, :] for i in range(count)] for t in tiles]
    for k in range(count):
        first = 8 * k
        in_block = (lane >= first) & (lane < first + 8)
        unit = jnp.where(lane == sub + first, 1.0, 0.0)
        for x in rows:
            block = x[k]
            cols = [jnp.broadcast_to(block[:, first + t:first + t + 1], (8, BLK)) for t in range(8)]
            forward = jnp.where(in_block, unit, block)
            jordan = forward
            inv = jnp.zeros((8, BLK), jnp.float32)
            piv = jnp.ones((8, BLK), jnp.float32)
            for j in range(8):
                d = jnp.broadcast_to(cols[j][j:j + 1, :], (8, BLK))
                r = 1.0 / d
                mult = jnp.where(sub == j, 0.0, cols[j] * r)
                for t in range(j + 1, 8):
                    cols[t] = cols[t] - mult * jnp.broadcast_to(cols[t][j:j + 1, :], (8, BLK))
                lead = jnp.broadcast_to(jordan[j:j + 1, :], (8, BLK))
                jordan = jordan - mult * lead
                if j < 7:
                    forward = forward - jnp.where(sub > j, mult, 0.0) * lead
                inv = jnp.where(sub == j, r, inv)
                piv = jnp.where(sub == j, d, piv)
            x[k] = forward * lax.rsqrt(piv)
            if k + 1 < count:
                z = jordan * inv
                zrow = [jnp.broadcast_to(z[t:t + 1, :], (8, BLK)) for t in range(8)]
                for i in range(k + 1, count):
                    held = x[i]
                    terms = [jnp.broadcast_to(held[:, first + t:first + t + 1], (8, BLK)) * zrow[t] for t in range(8)]
                    total = ((terms[0] + terms[1]) + (terms[2] + terms[3])) + ((terms[4] + terms[5]) + (terms[6] + terms[7]))
                    x[i] = jnp.where(in_block, 0.0, held) - total
    return [jnp.concatenate(x, axis=0) for x in rows]


def inverse_factor_kernel(gram_ref, out_ref):
    sectors, width, _ = out_ref.shape
    steps = width // BLK
    out_ref[...] = gram_ref[...]
    tri = lax.broadcasted_iota(jnp.int32, (BLK, BLK), 0) >= lax.broadcasted_iota(jnp.int32, (BLK, BLK), 1)
    row_at = lax.broadcasted_iota(jnp.int32, (BLK, width), 0)
    col_at = lax.broadcasted_iota(jnp.int32, (BLK, width), 1)

    def step(b, _):
        at = pl.multiple_of(b * BLK, BLK)
        here = pl.ds(at, BLK)
        done = factor_tile([out_ref[s, here, here] for s in range(sectors)])
        in_block = (col_at >= at) & (col_at < at + BLK)
        for s in range(sectors):
            low = jnp.where(tri, done[s], 0.0)
            panel = jnp.where(in_block, jnp.where(col_at == row_at + at, 1.0, 0.0), out_ref[s, here, :])
            out_ref[s, here, :] = jnp.dot(low, panel, precision=HI, preferred_element_type=jnp.float32)

        def trailing(i, _):
            below = pl.ds(pl.multiple_of(i * BLK, BLK), BLK)
            for s in range(sectors):
                left = out_ref[s, here, below]
                prod = lax.dot_general(left, out_ref[s, here, :], (((0,), (0,)), ((), ())), precision=HI, preferred_element_type=jnp.float32)
                out_ref[s, below, :] = jnp.where(in_block, 0.0, out_ref[s, below, :]) - prod
            return 0

        lax.fori_loop(b + 1, steps, trailing, 0)
        return 0

    lax.fori_loop(0, steps, step, 0)
    full = lax.broadcasted_iota(jnp.int32, (BLK, width), 1)
    for b in range(steps):
        for s in range(sectors):
            held = out_ref[s, b * BLK:(b + 1) * BLK, :]
            out_ref[s, b * BLK:(b + 1) * BLK, :] = jnp.where(full <= row_at + b * BLK, held, 0.0)


def inverse_factor(gram):
    sectors, width, _ = gram.shape
    return pl.pallas_call(
        inverse_factor_kernel,
        out_shape=jax.ShapeDtypeStruct(gram.shape, jnp.float32),
        in_specs=[pl.BlockSpec(memory_space=pltpu.VMEM)],
        out_specs=pl.BlockSpec(memory_space=pltpu.VMEM),
        compiler_params=pltpu.CompilerParams(vmem_limit_bytes=40 * 1024 * 1024),
        cost_estimate=pl.CostEstimate(flops=100_000_000_000, bytes_accessed=8 * gram.size, transcendentals=0),
        name="inverse_factor",
    )(gram)


def shards(theta, group_of, sector_sizes, row_order, omega):
    group_count = lax.axis_size("grp")
    group_slot = lax.axis_index("grp")
    per_group, cols, width = omega.shape
    sector_count, left_rows, _ = theta.shape
    sorted_ids = jnp.argsort(group_of, stable=True)
    widths_all = jnp.take(sector_sizes, sorted_ids)
    widths = lax.dynamic_slice_in_dim(widths_all, group_slot * per_group, per_group)
    local_rows = row_order % left_rows
    wanted = (sorted_ids[:, None] * left_rows + local_rows[None, :]).reshape(-1)
    pick = (wanted[:, None] == jnp.arange(sector_count * left_rows)[None, :]).astype(jnp.bfloat16)
    owned = jnp.dot(pick, theta.reshape(-1, cols), preferred_element_type=jnp.float32).astype(jnp.bfloat16)
    owned = owned.reshape(group_count, per_group, left_rows, cols)
    arrived = lax.all_to_all(owned, "grp", split_axis=0, concat_axis=2, tiled=True)
    sector_rows = arrived[0]
    sketch = jnp.einsum("src,sck->srk", sector_rows, omega, preferred_element_type=jnp.float32)
    live_cols = lax.broadcasted_iota(jnp.int32, (per_group, 1, width), 2) < widths[:, None, None]
    sketch = jnp.where(live_cols, sketch, 0.0)
    gram_local = jnp.einsum("srk,srj->skj", sketch, sketch, precision=HI, preferred_element_type=jnp.float32)
    gram_total = lax.psum(gram_local, "row")
    dead_diag = jnp.where(live_cols[:, 0, :], 0.0, 1.0)
    gram_total = gram_total + dead_diag[:, :, None] * jnp.eye(width, dtype=jnp.float32)[None]
    cross = jnp.einsum("src,srk->sck", sector_rows.astype(jnp.float32), sketch, precision=HI, preferred_element_type=jnp.float32)
    cross = lax.psum_scatter(cross, "row", scatter_dimension=1, tiled=True)
    inverse = inverse_factor(gram_total)
    basis = jnp.einsum("srk,sjk->srj", sketch, inverse, precision=HI, preferred_element_type=jnp.float32)
    core = jnp.einsum("sck,sjk->csj", cross, inverse, precision=HI, preferred_element_type=jnp.float32)
    return (basis, core)


def solution(mesh):
    return jax.shard_map(
        shards,
        mesh=mesh,
        in_specs=(P(None, ("row", "grp"), None), P(), P(), P(("row", "grp")), P("grp", None, None)),
        out_specs=(P("grp", "row", None), P("row", "grp", None)),
        check_vma=False,
    )
```

```python
import jax
import jax.numpy as jnp
from jax import lax
from jax.experimental import pallas as pl
from jax.experimental.pallas import tpu as pltpu
from jax.sharding import PartitionSpec as P

BLK = 128
STRIP = 256
HI = lax.Precision.HIGHEST


def factor_tile(tiles):
    sub = lax.broadcasted_iota(jnp.int32, (8, BLK), 0)
    lane = lax.broadcasted_iota(jnp.int32, (8, BLK), 1)
    count = BLK // 8
    rows = [[t[8 * i:8 * i + 8, :] for i in range(count)] for t in tiles]
    for k in range(count):
        first = 8 * k
        in_block = (lane >= first) & (lane < first + 8)
        unit = jnp.where(lane == sub + first, 1.0, 0.0)
        for x in rows:
            block = x[k]
            cols = [jnp.broadcast_to(block[:, first + t:first + t + 1], (8, BLK)) for t in range(8)]
            forward = jnp.where(in_block, unit, block)
            jordan = forward
            inv = jnp.zeros((8, BLK), jnp.float32)
            piv = jnp.ones((8, BLK), jnp.float32)
            for j in range(8):
                d = jnp.broadcast_to(cols[j][j:j + 1, :], (8, BLK))
                r = 1.0 / d
                mult = jnp.where(sub == j, 0.0, cols[j] * r)
                for t in range(j + 1, 8):
                    cols[t] = cols[t] - mult * jnp.broadcast_to(cols[t][j:j + 1, :], (8, BLK))
                lead = jnp.broadcast_to(jordan[j:j + 1, :], (8, BLK))
                jordan = jordan - mult * lead
                if j < 7:
                    forward = forward - jnp.where(sub > j, mult, 0.0) * lead
                inv = jnp.where(sub == j, r, inv)
                piv = jnp.where(sub == j, d, piv)
            x[k] = forward * lax.rsqrt(piv)
            if k + 1 < count:
                z = jordan * inv
                zrow = [jnp.broadcast_to(z[t:t + 1, :], (8, BLK)) for t in range(8)]
                for i in range(k + 1, count):
                    held = x[i]
                    terms = [jnp.broadcast_to(held[:, first + t:first + t + 1], (8, BLK)) * zrow[t] for t in range(8)]
                    total = ((terms[0] + terms[1]) + (terms[2] + terms[3])) + ((terms[4] + terms[5]) + (terms[6] + terms[7]))
                    x[i] = jnp.where(in_block, 0.0, held) - total
    return [jnp.concatenate(x, axis=0) for x in rows]


def inverse_factor_kernel(widths_ref, *refs):
    out_ref = refs[-1]
    packed = refs[:-1]
    sectors, width, _ = out_ref.shape
    steps = width // BLK
    for s in range(sectors):
        start = 0
        for at in range(0, width, STRIP):
            if at > 0:
                out_ref[s, at:at + STRIP, :at] = jnp.zeros((STRIP, at), jnp.float32)
            out_ref[s, at:at + STRIP, at:] = packed[s][:, start:start + width - at]
            start += width - at
    tile_row = lax.broadcasted_iota(jnp.int32, (BLK, BLK), 0)
    tile_col = lax.broadcasted_iota(jnp.int32, (BLK, BLK), 1)
    row_at = lax.broadcasted_iota(jnp.int32, (BLK, width), 0)
    col_at = lax.broadcasted_iota(jnp.int32, (BLK, width), 1)

    def step(b, _):
        at = pl.multiple_of(b * BLK, BLK)
        here = pl.ds(at, BLK)
        tiles = []
        for s in range(sectors):
            dead = (tile_row == tile_col) & (tile_row + at >= widths_ref[s])
            tiles.append(out_ref[s, here, here] + jnp.where(dead, 1.0, 0.0))
        done = factor_tile(tiles)
        in_block = (col_at >= at) & (col_at < at + BLK)
        for s in range(sectors):
            low = jnp.where(tile_row >= tile_col, done[s], 0.0)
            panel = jnp.where(in_block, jnp.where(col_at == row_at + at, 1.0, 0.0), out_ref[s, here, :])
            out_ref[s, here, :] = jnp.dot(low, panel, precision=HI, preferred_element_type=jnp.float32)

        def trailing(i, _):
            below = pl.ds(pl.multiple_of(i * BLK, BLK), BLK)
            for s in range(sectors):
                left = out_ref[s, here, below]
                prod = lax.dot_general(left, out_ref[s, here, :], (((0,), (0,)), ((), ())), precision=HI, preferred_element_type=jnp.float32)
                out_ref[s, below, :] = jnp.where(in_block, 0.0, out_ref[s, below, :]) - prod
            return 0

        lax.fori_loop(b + 1, steps, trailing, 0)
        return 0

    lax.fori_loop(0, steps, step, 0)
    for b in range(steps):
        for s in range(sectors):
            held = out_ref[s, b * BLK:(b + 1) * BLK, :]
            out_ref[s, b * BLK:(b + 1) * BLK, :] = jnp.where(col_at <= row_at + b * BLK, held, 0.0)


def inverse_factor(widths, packed, width):
    sectors = len(packed)
    return pl.pallas_call(
        inverse_factor_kernel,
        out_shape=jax.ShapeDtypeStruct((sectors, width, width), jnp.float32),
        in_specs=[pl.BlockSpec(memory_space=pltpu.SMEM)] + [pl.BlockSpec(memory_space=pltpu.VMEM)] * sectors,
        out_specs=pl.BlockSpec(memory_space=pltpu.VMEM),
        compiler_params=pltpu.CompilerParams(vmem_limit_bytes=40 * 1024 * 1024),
        cost_estimate=pl.CostEstimate(flops=100_000_000_000, bytes_accessed=8 * sectors * width * width, transcendentals=0),
        name="inverse_factor",
    )(widths, *packed)


def packed_gram(sketch):
    strips = []
    for at in range(0, sketch.shape[1], STRIP):
        strips.append(
            lax.dot_general(
                sketch[:, at:at + STRIP], sketch[:, at:], (((0,), (0,)), ((), ())), precision=HI, preferred_element_type=jnp.float32
            )
        )
    return jnp.concatenate(strips, axis=1)


def shards(theta, group_of, sector_sizes, row_order, omega):
    group_count = lax.axis_size("grp")
    group_slot = lax.axis_index("grp")
    per_group, cols, width = omega.shape
    sector_count, left_rows, _ = theta.shape
    sorted_ids = jnp.argsort(group_of, stable=True)
    widths_all = jnp.take(sector_sizes, sorted_ids)
    widths = lax.dynamic_slice_in_dim(widths_all, group_slot * per_group, per_group)
    local_rows = row_order % left_rows
    flat = theta.reshape(-1, cols)
    rows, sketches, grams = [], [], []
    for s in range(per_group):
        wanted = (sorted_ids[s::per_group][:, None] * left_rows + local_rows[None, :]).reshape(-1)
        pick = (wanted[:, None] == jnp.arange(sector_count * left_rows)[None, :]).astype(jnp.bfloat16)
        owned = jnp.dot(pick, flat, preferred_element_type=jnp.float32).astype(jnp.bfloat16)
        owned = owned.reshape(group_count, left_rows, cols)
        arrived = lax.all_to_all(owned, "grp", split_axis=0, concat_axis=0, tiled=True)
        arrived = arrived.reshape(group_count * left_rows, cols)
        sketch = jnp.dot(arrived, omega[s], preferred_element_type=jnp.float32)
        live = lax.broadcasted_iota(jnp.int32, (1, width), 1) < widths[s]
        sketch = jnp.where(live, sketch, 0.0)
        rows.append(arrived)
        sketches.append(sketch)
        packed = packed_gram(sketch)
        if grams:
            packed, grams[-1] = lax.optimization_barrier((packed, grams[-1]))
        grams.append(lax.psum(packed, "row"))
    cross = jnp.stack([
        lax.dot_general(
            r.astype(jnp.float32), k, (((0,), (0,)), ((), ())), precision=HI, preferred_element_type=jnp.float32
        )
        for r, k in zip(rows, sketches)
    ])
    cross, grams = lax.optimization_barrier((cross, grams))
    cross = lax.psum_scatter(cross, "row", scatter_dimension=1, tiled=True)
    inverse = inverse_factor(widths, grams, width)
    sketch = jnp.stack(sketches)
    basis = jnp.einsum("srk,sjk->srj", sketch, inverse, precision=HI, preferred_element_type=jnp.float32)
    core = jnp.einsum("sck,sjk->csj", cross, inverse, precision=HI, preferred_element_type=jnp.float32)
    return (basis, core)


def solution(mesh):
    return jax.shard_map(
        shards,
        mesh=mesh,
        in_specs=(P(None, ("row", "grp"), None), P(), P(), P(("row", "grp")), P("grp", None, None)),
        out_specs=(P("grp", "row", None), P("row", "grp", None)),
        check_vma=False,
    )
```

```python
import jax
import jax.numpy as jnp
from jax import lax
from jax.experimental import pallas as pl
from jax.experimental.pallas import tpu as pltpu
from jax.sharding import PartitionSpec as P

BLK = 128
STRIP = 256
HI = lax.Precision.HIGHEST


def factor_tile(tiles):
    sub = lax.broadcasted_iota(jnp.int32, (8, BLK), 0)
    lane = lax.broadcasted_iota(jnp.int32, (8, BLK), 1)
    count = BLK // 8
    rows = [[t[8 * i:8 * i + 8, :] for i in range(count)] for t in tiles]
    for k in range(count):
        first = 8 * k
        in_block = (lane >= first) & (lane < first + 8)
        unit = jnp.where(lane == sub + first, 1.0, 0.0)
        for x in rows:
            block = x[k]
            cols = [jnp.broadcast_to(block[:, first + t:first + t + 1], (8, BLK)) for t in range(8)]
            forward = jnp.where(in_block, unit, block)
            jordan = forward
            inv = jnp.zeros((8, BLK), jnp.float32)
            piv = jnp.ones((8, BLK), jnp.float32)
            for j in range(8):
                d = jnp.broadcast_to(cols[j][j:j + 1, :], (8, BLK))
                r = 1.0 / d
                mult = jnp.where(sub == j, 0.0, cols[j] * r)
                for t in range(j + 1, 8):
                    cols[t] = cols[t] - mult * jnp.broadcast_to(cols[t][j:j + 1, :], (8, BLK))
                lead = jnp.broadcast_to(jordan[j:j + 1, :], (8, BLK))
                jordan = jordan - mult * lead
                if j < 7:
                    forward = forward - jnp.where(sub > j, mult, 0.0) * lead
                inv = jnp.where(sub == j, r, inv)
                piv = jnp.where(sub == j, d, piv)
            x[k] = forward * lax.rsqrt(piv)
            if k + 1 < count:
                z = jordan * inv
                zrow = [jnp.broadcast_to(z[t:t + 1, :], (8, BLK)) for t in range(8)]
                for i in range(k + 1, count):
                    held = x[i]
                    terms = [jnp.broadcast_to(held[:, first + t:first + t + 1], (8, BLK)) * zrow[t] for t in range(8)]
                    total = ((terms[0] + terms[1]) + (terms[2] + terms[3])) + ((terms[4] + terms[5]) + (terms[6] + terms[7]))
                    x[i] = jnp.where(in_block, 0.0, held) - total
    return [jnp.concatenate(x, axis=0) for x in rows]


def inverse_factor_kernel(widths_ref, *refs):
    out_ref = refs[-1]
    packed = refs[:-1]
    sectors, width, _ = out_ref.shape
    steps = width // BLK
    for s in range(sectors):
        start = 0
        for at in range(0, width, STRIP):
            if at > 0:
                out_ref[s, at:at + STRIP, :at] = jnp.zeros((STRIP, at), jnp.float32)
            out_ref[s, at:at + STRIP, at:] = packed[s][:, start:start + width - at]
            start += width - at
    tile_row = lax.broadcasted_iota(jnp.int32, (BLK, BLK), 0)
    tile_col = lax.broadcasted_iota(jnp.int32, (BLK, BLK), 1)
    row_at = lax.broadcasted_iota(jnp.int32, (BLK, width), 0)
    col_at = lax.broadcasted_iota(jnp.int32, (BLK, width), 1)

    def step(b, _):
        at = pl.multiple_of(b * BLK, BLK)
        here = pl.ds(at, BLK)
        tiles = []
        for s in range(sectors):
            dead = (tile_row == tile_col) & (tile_row + at >= widths_ref[s])
            tiles.append(out_ref[s, here, here] + jnp.where(dead, 1.0, 0.0))
        done = factor_tile(tiles)
        in_block = (col_at >= at) & (col_at < at + BLK)
        for s in range(sectors):
            low = jnp.where(tile_row >= tile_col, done[s], 0.0)
            panel = jnp.where(in_block, jnp.where(col_at == row_at + at, 1.0, 0.0), out_ref[s, here, :])
            out_ref[s, here, :] = jnp.dot(low, panel, precision=HI, preferred_element_type=jnp.float32)

        def trailing(i, _):
            below = pl.ds(pl.multiple_of(i * BLK, BLK), BLK)
            for s in range(sectors):
                left = out_ref[s, here, below]
                prod = lax.dot_general(left, out_ref[s, here, :], (((0,), (0,)), ((), ())), precision=HI, preferred_element_type=jnp.float32)
                out_ref[s, below, :] = jnp.where(in_block, 0.0, out_ref[s, below, :]) - prod
            return 0

        lax.fori_loop(b + 1, steps, trailing, 0)
        return 0

    lax.fori_loop(0, steps, step, 0)
    for b in range(steps):
        for s in range(sectors):
            held = out_ref[s, b * BLK:(b + 1) * BLK, :]
            out_ref[s, b * BLK:(b + 1) * BLK, :] = jnp.where(col_at <= row_at + b * BLK, held, 0.0)


def inverse_factor(widths, packed, width):
    sectors = len(packed)
    return pl.pallas_call(
        inverse_factor_kernel,
        out_shape=jax.ShapeDtypeStruct((sectors, width, width), jnp.float32),
        in_specs=[pl.BlockSpec(memory_space=pltpu.SMEM)] + [pl.BlockSpec(memory_space=pltpu.VMEM)] * sectors,
        out_specs=pl.BlockSpec(memory_space=pltpu.VMEM),
        compiler_params=pltpu.CompilerParams(vmem_limit_bytes=40 * 1024 * 1024),
        cost_estimate=pl.CostEstimate(flops=100_000_000_000, bytes_accessed=8 * sectors * width * width, transcendentals=0),
        name="inverse_factor",
    )(widths, *packed)


def packed_gram(sketch):
    strips = []
    for at in range(0, sketch.shape[1], STRIP):
        strips.append(
            lax.dot_general(
                sketch[:, at:at + STRIP], sketch[:, at:], (((0,), (0,)), ((), ())), precision=HI, preferred_element_type=jnp.float32
            )
        )
    return jnp.concatenate(strips, axis=1)


def halving_sum(part, order):
    size = lax.axis_size("row")
    me = lax.axis_index("row")
    for bit in order:
        half = part.shape[0] // 2
        mine = (me >> bit) & 1
        pairs = [(i, i ^ (1 << bit)) for i in range(size)]
        keep = lax.dynamic_slice_in_dim(part, mine * half, half)
        give = lax.dynamic_slice_in_dim(part, (1 - mine) * half, half)
        part = keep + lax.ppermute(give, "row", pairs)
    for bit in reversed(order):
        mine = (me >> bit) & 1
        pairs = [(i, i ^ (1 << bit)) for i in range(size)]
        other = lax.ppermute(part, "row", pairs)
        low = jnp.where(mine == 0, part, other)
        high = jnp.where(mine == 0, other, part)
        part = jnp.concatenate([low, high], axis=0)
    return part


def row_sum(packed):
    size = lax.axis_size("row")
    bits = size.bit_length() - 1
    if size != 1 << bits:
        return lax.psum(packed, "row")
    half = packed.shape[0] // 2
    inner = list(range(1, bits))
    return jnp.concatenate([halving_sum(packed[:half], [0] + inner), halving_sum(packed[half:], [0] + inner[::-1])], axis=0)


def shards(theta, group_of, sector_sizes, row_order, omega):
    group_count = lax.axis_size("grp")
    group_slot = lax.axis_index("grp")
    per_group, cols, width = omega.shape
    sector_count, left_rows, _ = theta.shape
    sorted_ids = jnp.argsort(group_of, stable=True)
    widths_all = jnp.take(sector_sizes, sorted_ids)
    widths = lax.dynamic_slice_in_dim(widths_all, group_slot * per_group, per_group)
    local_rows = row_order % left_rows
    flat = theta.reshape(-1, cols)
    rows, sketches, grams = [], [], []
    for s in range(per_group):
        wanted = (sorted_ids[s::per_group][:, None] * left_rows + local_rows[None, :]).reshape(-1)
        pick = (wanted[:, None] == jnp.arange(sector_count * left_rows)[None, :]).astype(jnp.bfloat16)
        owned = jnp.dot(pick, flat, preferred_element_type=jnp.float32).astype(jnp.bfloat16)
        owned = owned.reshape(group_count, left_rows, cols)
        arrived = lax.all_to_all(owned, "grp", split_axis=0, concat_axis=0, tiled=True)
        arrived = arrived.reshape(group_count * left_rows, cols)
        sketch = jnp.dot(arrived, omega[s], preferred_element_type=jnp.float32)
        live = lax.broadcasted_iota(jnp.int32, (1, width), 1) < widths[s]
        sketch = jnp.where(live, sketch, 0.0)
        rows.append(arrived)
        sketches.append(sketch)
        grams.append(row_sum(packed_gram(sketch)))
    cross = jnp.stack([
        lax.dot_general(
            r.astype(jnp.float32), k, (((0,), (0,)), ((), ())), precision=HI, preferred_element_type=jnp.float32
        )
        for r, k in zip(rows, sketches)
    ])
    cross, grams = lax.optimization_barrier((cross, grams))
    cross = lax.psum_scatter(cross, "row", scatter_dimension=1, tiled=True)
    inverse = inverse_factor(widths, grams, width)
    sketch = jnp.stack(sketches)
    basis = jnp.einsum("srk,sjk->srj", sketch, inverse, precision=HI, preferred_element_type=jnp.float32)
    core = jnp.einsum("sck,sjk->csj", cross, inverse, precision=HI, preferred_element_type=jnp.float32)
    return (basis, core)


def solution(mesh):
    return jax.shard_map(
        shards,
        mesh=mesh,
        in_specs=(P(None, ("row", "grp"), None), P(), P(), P(("row", "grp")), P("grp", None, None)),
        out_specs=(P("grp", "row", None), P("row", "grp", None)),
        check_vma=False,
    )
```
